32 devices in a mesh: width: 4 (over x, core), hidden: 8 (over z, y).
Axes of the slice: x: 2, y: 2, z: 4, core: 2. Of those that a mesh axis runs over, the one named last changes fastest.
Arguments:
- inputs: bfloat16 [512, 6144], P(None, 'width'), may hold values from -6 to 6
- weight_in: bfloat16 [6144, 16384], P('width', 'hidden'), may hold values from -0.078125 to 0.078125
- weight_out: bfloat16 [16384, 6144], P('hidden', 'width'), may hold values from -0.046875 to 0.046875
- gradient_in: bfloat16 [6144, 16384], P('width', 'hidden'), may hold values from -10.4 to 10.4
- gradient_out: bfloat16 [16384, 6144], P('hidden', 'width'), may hold values from -10.4 to 10.4
- left_in: bfloat16 [6144, 384], P('width'), may hold values from -5 to 7, as said below
- right_in: bfloat16 [16384, 256], P('hidden'), may hold values from -5 to 7, as said below
- left_out: bfloat16 [16384, 256], P('hidden'), may hold values from -5 to 7, as said below
- right_out: bfloat16 [6144, 384], P('width'), may hold values from -5 to 7, as said below
- damping: float32 [1], replicated, may hold values from 0.5 to 2
Outputs:
- step_in: float32 [6144, 16384], P('width', 'hidden')
- step_out: float32 [16384, 6144], P('hidden', 'width')
- res_in: float32 [6144, 16384], P('width', 'hidden')
- res_out: float32 [16384, 6144], P('hidden', 'width')
The draws below stay inside these ranges and needn't reach their ends.
Inputs may be any that keep to these rules, and one draw needn't show every extreme that they name: `left_in`: each aligned block of 384 rows is one symmetric positive definite 384 x 384 matrix. `right_in`: each aligned block of 256 rows is one symmetric positive definite 256 x 256 matrix. `left_out`: each aligned block of 256 rows is one symmetric positive definite 256 x 256 matrix. `right_out`: each aligned block of 384 rows is one symmetric positive definite 384 x 384 matrix.
All inputs are finite; a program needn't handle non-finite values.
Results may differ from the reference program's by a relative error of at most 0.025.
Values may be sent and summed in bfloat16 or wider, within the bound.
A program may use at most 256 MiB of HBM per device.

```python
import math
import jax
import jax.numpy as jnp
from jax import lax

D = 6144
FF = 16384
BD = 384
BF = 256
ITERS = 2
TOKENS = 512


def block_factor(key, row_total, block_size):
    block_count = row_total // block_size
    matrix_key, diagonal_key = jax.random.split(key)
    matrix = jnp.clip(jax.random.normal(matrix_key, (block_count, block_size, block_size), jnp.float32), -3.0, 3.0)
    diagonal = jnp.exp(jax.random.uniform(diagonal_key, (block_count, block_size), jnp.float32, -0.6931472, 0.6931472))
    gram = jnp.einsum('kab,kcb->kac', matrix, matrix) * (0.5 / block_size)
    identity = jnp.eye(block_size, dtype=jnp.float32)
    blocks = gram + identity[None, :, :] * diagonal[:, :, None]
    return blocks.reshape(row_total, block_size).astype(jnp.bfloat16)


def rising_field(key, row_total, col_total, row_weight, col_weight):
    row_place = jnp.arange(row_total, dtype=jnp.float32)[:, None] / row_total
    col_place = jnp.arange(col_total, dtype=jnp.float32)[None, :] / col_total
    level = row_weight * row_place + col_weight * col_place
    noise = jnp.clip(jax.random.normal(key, (row_total, col_total), jnp.float32), -6.0, 6.0)
    scales = jnp.sqrt(1.0 + 2.0 * level)
    return (noise * scales).astype(jnp.bfloat16)


def draw_gradient_in(key, part):
    return rising_field(jax.random.fold_in(key, 21), D, FF, 0.9, 0.1)


def draw_gradient_out(key, part):
    return rising_field(jax.random.fold_in(key, 22), FF, D, 0.1, 0.9)


def draw_left_in(key, part):
    return block_factor(jax.random.fold_in(key, 11), D, BD)


def draw_right_in(key, part):
    return block_factor(jax.random.fold_in(key, 12), FF, BF)


def draw_left_out(key, part):
    return block_factor(jax.random.fold_in(key, 13), FF, BF)


def draw_right_out(key, part):
    return block_factor(jax.random.fold_in(key, 14), D, BD)


def block_levels(stream_key, extent, pieces, low, top_value):
    def one(axis_at, shards_of):
        heights = jax.random.uniform(jax.random.fold_in(jax.random.fold_in(stream_key, 6), axis_at), (shards_of,), jnp.float32, low / len(pieces), top_value / len(pieces))
        return jnp.repeat(jnp.exp(heights), extent[axis_at] // shards_of).reshape((-1,) + (1,) * (len(extent) - axis_at - 1))

    factor_of = one(*pieces[0])
    for cut in pieces[1:]:
        factor_of = factor_of * one(*cut)
    return factor_of


def normal_values(stream_key, shape, deviation, reach, shards=(), kind=jnp.bfloat16):
    values = deviation * jax.random.normal(stream_key, shape, jnp.float32)
    if shards:
        values = values * block_levels(stream_key, shape, shards, -0.22, 0.18)
    return jnp.clip(values, -reach, reach).astype(kind)


def setup_inputs(seed: int = 0) -> dict:
    streams_of = jax.random.split(jax.random.key(seed), 11)
    return {
        "inputs": normal_values(streams_of[0], (TOKENS, D), 1.0, 6.0, ((1, 4),)),
        "weight_in": normal_values(streams_of[1], (D, FF), D ** -0.5, 0.078125, ((0, 4), (1, 8))),
        "weight_out": normal_values(streams_of[2], (FF, D), FF ** -0.5, 0.046875, ((0, 8), (1, 4))),
        "gradient_in": draw_gradient_in(jax.random.fold_in(streams_of[10], 71), 0),
        "gradient_out": draw_gradient_out(jax.random.fold_in(streams_of[10], 71), 0),
        "left_in": draw_left_in(jax.random.fold_in(streams_of[10], 71), 0),
        "right_in": draw_right_in(jax.random.fold_in(streams_of[10], 71), 0),
        "left_out": draw_left_out(jax.random.fold_in(streams_of[10], 71), 0),
        "right_out": draw_right_out(jax.random.fold_in(streams_of[10], 71), 0),
        "damping": jnp.clip(jnp.exp(jax.random.uniform(streams_of[9], (1,), jnp.float32, math.log(0.5), math.log(2.0))), 0.5, 2.0),
    }


HIGHEST_PRECISION = lax.Precision.HIGHEST


def activate(pre_act):
    normal_cdf = 0.5 * (1.0 + lax.erf(pre_act * 0.7071067811865476))
    activation = (pre_act * normal_cdf).astype(jnp.bfloat16)
    slopes = (normal_cdf + pre_act * jnp.exp(-0.5 * pre_act * pre_act) * 0.3989422804014327).astype(jnp.bfloat16)
    return activation, slopes


def left_apply(blocks, matrix, block_size):
    row_total, col_total = matrix.shape
    stacked = blocks.astype(jnp.float32).reshape(row_total // block_size, block_size, block_size)
    shaped = matrix.reshape(row_total // block_size, block_size, col_total)
    product = jnp.einsum("kab,kbc->kac", stacked, shaped, precision=HIGHEST_PRECISION)
    return product.reshape(row_total, col_total)


def right_apply(blocks, matrix, block_size):
    row_total, col_total = matrix.shape
    stacked = blocks.astype(jnp.float32).reshape(col_total // block_size, block_size, block_size)
    shaped = matrix.reshape(row_total, col_total // block_size, block_size)
    product = jnp.einsum("rkb,kbc->rkc", shaped, stacked, precision=HIGHEST_PRECISION)
    return product.reshape(row_total, col_total)


def reference(inputs, weight_in, weight_out, gradient_in, gradient_out, left_in, right_in, left_out, right_out, damping):
    pre_act = jnp.dot(inputs, weight_in, preferred_element_type=jnp.float32)
    activation, slopes = activate(pre_act)
    damper = damping[0]

    def precondition(first_part, second_part):
        first_new = right_apply(right_in, left_apply(left_in, first_part, BD), BF)
        second_new = right_apply(right_out, left_apply(left_out, second_part, BF), BD)
        return first_new, second_new

    def curvature(vector_in, vector_out):
        tan_pre = jnp.dot(inputs, vector_in.astype(jnp.bfloat16), preferred_element_type=jnp.float32)
        tan_act = (slopes * tan_pre).astype(jnp.bfloat16)
        out_sum = jnp.dot(tan_act, weight_out, preferred_element_type=jnp.float32)
        out_sum = out_sum + jnp.dot(activation, vector_out.astype(jnp.bfloat16), preferred_element_type=jnp.float32)
        errors = (out_sum / TOKENS).astype(jnp.bfloat16)
        back_act = jnp.dot(errors, weight_out.T, preferred_element_type=jnp.float32)
        back_pre = (slopes * back_act).astype(jnp.bfloat16)
        image_in = jnp.dot(inputs.T, back_pre, preferred_element_type=jnp.float32) + damper * vector_in
        image_out = jnp.dot(activation.T, errors, preferred_element_type=jnp.float32) + damper * vector_out
        return image_in, image_out

    res_in = gradient_in.astype(jnp.float32)
    res_out = gradient_out.astype(jnp.float32)
    step_in = jnp.zeros_like(res_in)
    step_out = jnp.zeros_like(res_out)
    precond_in, precond_out = precondition(res_in, res_out)
    norm_now = jnp.sum(res_in * precond_in) + jnp.sum(res_out * precond_out)
    search_in, search_out = precond_in, precond_out
    for iteration in range(ITERS):
        image_in, image_out = curvature(search_in, search_out)
        step_size = norm_now / (jnp.sum(search_in * image_in) + jnp.sum(search_out * image_out))
        step_in = step_in + step_size * search_in
        step_out = step_out + step_size * search_out
        res_in = res_in - step_size * image_in
        res_out = res_out - step_size * image_out
        if iteration + 1 < ITERS:
            precond_in, precond_out = precondition(res_in, res_out)
            norm_next = jnp.sum(res_in * precond_in) + jnp.sum(res_out * precond_out)
            momentum = norm_next / norm_now
            search_in = precond_in + momentum * search_in
            search_out = precond_out + momentum * search_out
            norm_now = norm_next
    return step_in, step_out, res_in, res_out
```

```python
import functools

import jax
import jax.numpy as jnp
from jax import lax
from jax.experimental import pallas as pl
from jax.experimental.pallas import tpu as pltpu
from jax.sharding import PartitionSpec as P

BF16 = jnp.bfloat16
F32 = jnp.float32


def dot32(a, b):
    return jnp.dot(a, b, preferred_element_type=F32)


def largest(total, *choices):
    for choice in choices:
        if total % choice == 0:
            return choice
    return total


def fold(values):
    rows, cols = values.shape
    part = values.reshape(rows // 8, 8, cols).sum(axis=0)
    total = part[:, :128]
    for at in range(128, cols, 128):
        total = total + part[:, at : at + 128]
    return total


def params():
    return pltpu.CompilerParams(vmem_limit_bytes=48 * 1024 * 1024)


def krylov_kernel(chunks, left_ref, right_ref, grad_ref, first_ref, second_ref, stat_ref):
    @pl.when((pl.program_id(0) == 0) & (pl.program_id(1) == 0))
    def _():
        stat_ref[...] = jnp.zeros_like(stat_ref)

    left = left_ref[...]
    size = right_ref.shape[1]
    places = [slice(at * size, (at + 1) * size) for at in range(chunks)]
    half = dot32(left, grad_ref[...]).astype(BF16)
    for place in places:
        first = dot32(half[:, place], right_ref[place, :])
        first_ref[:, place] = first.astype(BF16)
        stat_ref[0:8, :] += fold(grad_ref[:, place].astype(F32) * first)
        stat_ref[8:16, :] += fold(first * first)
    half = dot32(left, first_ref[...]).astype(BF16)
    for place in places:
        second = dot32(half[:, place], right_ref[place, :])
        second_ref[:, place] = second.astype(BF16)
        stat_ref[16:24, :] += fold(first_ref[:, place].astype(F32) * second)
        stat_ref[24:32, :] += fold(second * second)


def krylov(left, right, grad):
    rows, cols = grad.shape
    left_size, right_size = left.shape[1], right.shape[1]
    chunks = largest(cols // right_size, 4, 2, 1)
    wide = chunks * right_size
    tile = pl.BlockSpec((left_size, wide), lambda j, k: (k, j))
    return pl.pallas_call(
        functools.partial(krylov_kernel, chunks),
        grid=(cols // wide, rows // left_size),
        in_specs=[
            pl.BlockSpec((left_size, left_size), lambda j, k: (k, 0)),
            pl.BlockSpec((wide, right_size), lambda j, k: (j, 0)),
            tile,
        ],
        out_specs=[tile, tile, pl.BlockSpec((32, 128), lambda j, k: (0, 0))],
        out_shape=[
            jax.ShapeDtypeStruct(grad.shape, BF16),
            jax.ShapeDtypeStruct(grad.shape, BF16),
            jax.ShapeDtypeStruct((32, 128), F32),
        ],
        compiler_params=params(),
        cost_estimate=pl.CostEstimate(
            flops=4 * rows * cols * (left_size + right_size),
            bytes_accessed=6 * rows * cols,
            transcendentals=0,
        ),
        name="krylov",
    )(left, right, grad)


def image_kernel(first_ref, token_ref, second_ref, out_ref, stat_ref):
    @pl.when((pl.program_id(0) == 0) & (pl.program_id(1) == 0))
    def _():
        stat_ref[...] = jnp.zeros_like(stat_ref)

    image = dot32(first_ref[...], token_ref[...])
    out_ref[...] = image.astype(BF16)
    stat_ref[0:8, :] += fold(image * image)
    stat_ref[8:16, :] += fold(image * second_ref[...].astype(F32))


def image(first, tokens, second):
    rows, cols = second.shape
    count = tokens.shape[0]
    high = largest(rows, 512, 384, 256)
    wide = largest(cols, 1024, 768, 512)
    tile = pl.BlockSpec((high, wide), lambda j, i: (i, j))
    return pl.pallas_call(
        image_kernel,
        grid=(cols // wide, rows // high),
        in_specs=[
            pl.BlockSpec((high, count), lambda j, i: (i, 0)),
            pl.BlockSpec((count, wide), lambda j, i: (0, j)),
            tile,
        ],
        out_specs=[tile, pl.BlockSpec((16, 128), lambda j, i: (0, 0))],
        out_shape=[
            jax.ShapeDtypeStruct(second.shape, BF16),
            jax.ShapeDtypeStruct((16, 128), F32),
        ],
        compiler_params=params(),
        cost_estimate=pl.CostEstimate(
            flops=2 * rows * cols * count, bytes_accessed=4 * rows * cols, transcendentals=0
        ),
        name="image",
    )(first, tokens, second)


def right_kernel(token_ref, right_ref, out_ref):
    out_ref[...] = dot32(token_ref[...], right_ref[...]).astype(BF16)


def right_apply(tokens, right):
    count, cols = tokens.shape
    size = right.shape[1]
    tile = pl.BlockSpec((count, size), lambda j: (0, j))
    return pl.pallas_call(
        right_kernel,
        grid=(cols // size,),
        in_specs=[tile, pl.BlockSpec((size, size), lambda j: (j, 0))],
        out_specs=tile,
        out_shape=jax.ShapeDtypeStruct(tokens.shape, BF16),
        compiler_params=params(),
        cost_estimate=pl.CostEstimate(
            flops=2 * count * cols * size, bytes_accessed=4 * count * cols, transcendentals=0
        ),
        name="right_apply",
    )(tokens, right)


def step_kernel(scale_ref, first_ref, second_ref, image_ref, grad_ref, step_ref, rest_ref):
    c0, c1, c2, damper = (scale_ref[at : at + 1, 0:1] for at in range(4))
    step = (
        c0 * first_ref[...].astype(F32)
        + c1 * second_ref[...].astype(F32)
        + c2 * image_ref[...].astype(F32)
    )
    step_ref[...] = step
    rest_ref[...] = (grad_ref[...].astype(F32) - damper * step).astype(BF16)


def make_step(scales, first, second, image_of, grad):
    rows, cols = grad.shape
    high = largest(rows, 256, 128)
    tile = pl.BlockSpec((high, cols), lambda i: (i, 0))
    return pl.pallas_call(
        step_kernel,
        grid=(rows // high,),
        in_specs=[pl.BlockSpec((8, 128), lambda i: (0, 0))] + [tile] * 4,
        out_specs=[tile, tile],
        out_shape=[
            jax.ShapeDtypeStruct(grad.shape, F32),
            jax.ShapeDtypeStruct(grad.shape, BF16),
        ],
        compiler_params=params(),
        cost_estimate=pl.CostEstimate(
            flops=8 * rows * cols, bytes_accessed=14 * rows * cols, transcendentals=0
        ),
        name="make_step",
    )(scales, first, second, image_of, grad)


def whole_sum(values):
    return jnp.sum(jnp.sum(values, axis=0, keepdims=True), axis=1, keepdims=True)


def sums_kernel(in_ref, out_ref, more_in_ref, more_out_ref, u0_ref, u1_ref, u2_ref, sums_ref):
    stats = in_ref[...] + out_ref[...]
    more = more_in_ref[...] + more_out_ref[...]
    parts = [stats[at : at + 8, :] for at in range(0, 32, 8)]
    parts += [more[at : at + 8, :] for at in range(0, 16, 8)]
    rows = [ref[...].astype(F32) for ref in (u0_ref, u1_ref, u2_ref)]
    parts += [fold(rows[a] * rows[b]) for a in range(3) for b in range(a, 3)]
    sums_ref[...] = jnp.zeros_like(sums_ref)
    for at, part in enumerate(parts):
        sums_ref[at : at + 1, :] = jnp.broadcast_to(whole_sum(part), (1, 128))


def local_sums(stats, rows):
    return pl.pallas_call(
        sums_kernel,
        out_shape=jax.ShapeDtypeStruct((16, 128), F32),
        compiler_params=params(),
        name="local_sums",
    )(*stats, *rows)


def mix_kernel(tokens, sums_ref, damp_ref, u0_ref, u1_ref, u2_ref, scale_ref, share_ref):
    sums = [sums_ref[at : at + 1, :] for at in range(12)]
    damper = damp_ref[...]
    norm, ff, fs, ss, ii, si = sums[:6]
    g00, g01, g02, g11, g12, g22 = (value / tokens for value in sums[6:])
    size_one = norm / (g00 + damper * ff)
    norm_next = size_one * size_one * (g02 + 2.0 * damper * g01 + damper * damper * fs) - norm
    d0 = 1.0 + norm_next / norm
    d1 = -size_one * damper
    d2 = -size_one
    curved = (
        d0 * d0 * g00
        + d1 * d1 * g11
        + d2 * d2 * g22
        + 2.0 * (d0 * d1 * g01 + d0 * d2 * g02 + d1 * d2 * g12)
    )
    square = (
        d0 * d0 * ff
        + d1 * d1 * ss
        + d2 * d2 * ii
        + 2.0 * (d0 * d1 * fs + d0 * d2 * g01 + d1 * d2 * si)
    )
    size_two = norm_next / (curved + damper * square)
    found = [size_one + size_two * d0, size_two * d1, size_two * d2]
    scale_ref[...] = jnp.zeros_like(scale_ref)
    for at, value in enumerate(found + [damper]):
        scale_ref[at : at + 1, :] = value
    c0, c1, c2 = (value[:, 0:1] for value in found)
    mixed = (
        c0 * u0_ref[...].astype(F32) + c1 * u1_ref[...].astype(F32) + c2 * u2_ref[...].astype(F32)
    )
    share_ref[...] = (mixed / tokens).astype(BF16)


def mix(tokens, sums, damp_row, rows):
    return pl.pallas_call(
        functools.partial(mix_kernel, tokens),
        out_shape=[
            jax.ShapeDtypeStruct((8, 128), F32),
            jax.ShapeDtypeStruct(rows[0].shape, BF16),
        ],
        compiler_params=params(),
        name="mix",
    )(sums, damp_row, *rows)


def residual_kernel(first_ref, token_ref, rest_ref, out_ref):
    out_ref[...] = rest_ref[...].astype(F32) - dot32(first_ref[...], token_ref[...])


def residual(first, tokens, rest):
    rows, cols = rest.shape
    count = tokens.shape[0]
    high = largest(rows, 512, 384, 256)
    wide = largest(cols, 1024, 768, 512)
    tile = pl.BlockSpec((high, wide), lambda j, i: (i, j))
    return pl.pallas_call(
        residual_kernel,
        grid=(cols // wide, rows // high),
        in_specs=[
            pl.BlockSpec((high, count), lambda j, i: (i, 0)),
            pl.BlockSpec((count, wide), lambda j, i: (0, j)),
            tile,
        ],
        out_specs=tile,
        out_shape=jax.ShapeDtypeStruct(rest.shape, F32),
        compiler_params=params(),
        cost_estimate=pl.CostEstimate(
            flops=2 * rows * cols * count, bytes_accessed=6 * rows * cols, transcendentals=0
        ),
        name="residual",
    )(first, tokens, rest)


def activate(pre_act):
    normal_cdf = 0.5 * (1.0 + lax.erf(pre_act * 0.7071067811865476))
    activation = (pre_act * normal_cdf).astype(BF16)
    slopes = (normal_cdf + pre_act * jnp.exp(-0.5 * pre_act * pre_act) * 0.3989422804014327).astype(
        BF16
    )
    return activation, slopes


def left_apply(left, matrix):
    rows, cols = matrix.shape
    size = left.shape[1]
    product = jnp.einsum(
        "kab,kbc->kac",
        left.reshape(rows // size, size, size),
        matrix.reshape(rows // size, size, cols),
        preferred_element_type=F32,
    )
    return product.astype(BF16).reshape(rows, cols)


def swap(values, axis, bit):
    count = lax.axis_size(axis)
    return lax.ppermute(values, axis, [(at, at ^ bit) for at in range(count)])


def is_upper(axis, bit):
    return (lax.axis_index(axis) & bit) != 0


def add_low(first, second):
    return (first.astype(F32) + second.astype(F32)).astype(BF16)


def bits_of(axis):
    count = lax.axis_size(axis)
    bits, bit = [], 1
    while bit < count:
        bits.append(bit)
        bit *= 2
    return bits


def halve(values, axis, bit, dim):
    low, high = jnp.split(values, 2, axis=dim)
    upper = is_upper(axis, bit)
    kept = jnp.where(upper, high, low)
    return add_low(kept, swap(jnp.where(upper, low, high), axis, bit))


def double(values, axis, bit, dim):
    other = swap(values, axis, bit)
    upper = is_upper(axis, bit)
    return jnp.concatenate(
        [jnp.where(upper, other, values), jnp.where(upper, values, other)], axis=dim
    )


def over_width(partial, cover=(), late=None):
    values = partial.astype(BF16)
    near, *far = bits_of("width")
    values = halve(values, "width", near, 1)
    if late is not None:
        values, late = lax.optimization_barrier((values, late))
        cover = (late,)
    for bit in far:
        values = add_low(values, swap(values, "width", bit))
    if cover and late is None:
        values, *cover = lax.optimization_barrier((values, *cover))
    return double(values, "width", near, 1), cover


def orders():
    bits = bits_of("hidden")
    return bits, bits[1:] + bits[:1]


def scatter(partial):
    pieces = []
    for values, order in zip(jnp.split(partial.astype(BF16), 2, axis=1), orders()):
        for bit in order:
            values = halve(values, "hidden", bit, 0)
        pieces.append(values)
    return jnp.concatenate(pieces, axis=1)


def gather(rows):
    pieces = []
    for values, order in zip(jnp.split(rows, 2, axis=1), orders()):
        for bit in order[::-1]:
            values = double(values, "hidden", bit, 0)
        pieces.append(values)
    return jnp.concatenate(pieces, axis=1)


def over_all(values):
    for axis in ("width", "hidden"):
        for bit in bits_of(axis):
            values = values + swap(values, axis, bit)
    return values


def body(
    inputs,
    weight_in,
    weight_out,
    gradient_in,
    gradient_out,
    left_in,
    right_in,
    left_out,
    right_out,
    damping,
):
    tokens = inputs.shape[0]
    damper = damping[0]

    pre_act, (left_late,) = over_width(dot32(inputs, weight_in), late=left_in)
    pre_act = pre_act.astype(F32)
    first_in, second_in, stat_in = krylov(left_late, right_in, gradient_in)
    tan_first, (first_out, second_out, stat_out) = over_width(
        dot32(inputs, first_in), krylov(left_out, right_out, gradient_out)
    )
    inputs_t = inputs.T
    mixed_in = left_apply(left_in, inputs_t)
    token_in, _ = over_width(
        lax.dot_general(mixed_in, inputs_t, (((0,), (0,)), ((), ())), preferred_element_type=F32)
    )

    activation, slopes = activate(pre_act)
    slopes_wide = slopes.astype(F32)
    act_first = (slopes_wide * tan_first.astype(F32)).astype(BF16)
    whole_first = (dot32(act_first, weight_out) + dot32(activation, first_out)).astype(BF16)
    whole_first, late_in = lax.optimization_barrier((whole_first, second_in))
    rows_first = scatter(whole_first)
    errors = gather((rows_first.astype(F32) / tokens).astype(BF16))
    tan_second, _ = over_width(dot32(inputs, late_in))
    act_second = (slopes_wide * tan_second.astype(F32)).astype(BF16)
    rows_second = scatter(dot32(act_second, weight_out) + dot32(activation, second_out))
    activation_t = activation.T
    mixed_out = left_apply(left_out, activation_t)
    token_out = lax.dot_general(
        mixed_out, activation_t, (((0,), (0,)), ((), ())), preferred_element_type=F32
    ).astype(BF16)

    def pull_back(rows, cover):
        product = lax.dot_general(
            rows, weight_out, (((1,), (1,)), ((), ())), preferred_element_type=F32
        )
        total, cover = over_width(product, cover)
        return (slopes_wide * total.astype(F32)).astype(BF16), cover

    errors_right = right_apply(errors, right_out)
    back, (image_out, more_out) = pull_back(errors, image(mixed_out, errors_right, second_out))
    back_right = right_apply(back, right_in)
    act_third = (slopes_wide * dot32(token_in, back_right)).astype(BF16)
    third = (dot32(act_third, weight_out) + dot32(token_out, errors_right)).astype(BF16)
    third, late_right = lax.optimization_barrier((third, back_right))
    rows_third = scatter(third)
    image_in, more_in = image(mixed_in, late_right, second_in)

    sums = over_all(
        local_sums((stat_in, stat_out, more_in, more_out), (rows_first, rows_second, rows_third))
    )
    damp_row = jnp.full((1, 128), damper, F32)
    scales, share = mix(tokens, sums, damp_row, (rows_first, rows_second, rows_third))
    total_errors = gather(share)
    step_in, rest_in = make_step(scales, first_in, second_in, image_in, gradient_in)
    step_out, rest_out = make_step(scales, first_out, second_out, image_out, gradient_out)
    total_back, (step_in, step_out, rest_in, rest_out) = pull_back(
        total_errors, (step_in, step_out, rest_in, rest_out)
    )
    res_out = residual(activation_t, total_errors, rest_out)
    res_in = residual(inputs_t, total_back, rest_in)
    return step_in, step_out, res_in, res_out


def solution(mesh):
    return jax.shard_map(
        body,
        mesh=mesh,
        in_specs=(
            P(None, "width"),
            P("width", "hidden"),
            P("hidden", "width"),
            P("width", "hidden"),
            P("hidden", "width"),
            P("width", None),
            P("hidden", None),
            P("hidden", None),
            P("width", None),
            P(),
        ),
        out_specs=(
            P("width", "hidden"),
            P("hidden", "width"),
            P("width", "hidden"),
            P("hidden", "width"),
        ),
        check_vma=False,
    )
```
